32 devices in a mesh: blk: 8 (over z, y), rep: 4 (over x, core).
Axes of the slice: x: 2, y: 2, z: 4, core: 2. Of those that a mesh axis runs over, the one named last changes fastest.
Arguments:
- resident_keys: int32 [16384], P('blk'), may hold values from 0 to 4095
- moving_keys: int32 [65536], P(('blk', 'rep')), may hold values from 0 to 4095
- payload: float32 [65536, 128], P(('blk', 'rep')), may hold values from -6 to 6
Outputs:
- joined: float32 [16384, 128], P(('blk', 'rep'))
The draws below stay inside these ranges and needn't reach their ends.
All inputs are finite; a program needn't handle non-finite values.
Results may differ from the reference program's by a relative error of at most 0.0003.
Values sent between devices are 32-bit elements; how exact they have to be, the bound alone decides.
A program may use at most 64 MiB of HBM per device.

```python
import jax
import jax.numpy as jnp
from jax import lax

R_DEV = 2048
S_DEV = 2048
P_SIZE = 128
KEYS = 4096
REACH = 2
R_ROWS = 16384
S_ROWS = 65536
N_BLK = 8
N_REP = 4


def place_ends(array, stream_key, least, high):
    spot = [jax.random.randint(jax.random.fold_in(stream_key, axis), (), 0, length) for axis, length in enumerate(array.shape)]
    main_axis = array.shape.index(max(array.shape))
    neighbour = spot[:main_axis] + [(spot[main_axis] + 1) % array.shape[main_axis]] + spot[main_axis + 1:]
    return array.at[tuple(spot)].set(least).at[tuple(neighbour)].set(high)


def block_scale(stream_key, shape, pieces, least, high):
    def one(position, shards_of):
        heights = jax.random.uniform(jax.random.fold_in(jax.random.fold_in(stream_key, 6), position), (shards_of,), jnp.float32, least / len(pieces), high / len(pieces))
        return jnp.repeat(jnp.exp(heights), shape[position] // shards_of).reshape((-1,) + (1,) * (len(shape) - position - 1))

    level = one(*pieces[0])
    for cut in pieces[1:]:
        level = level * one(*cut)
    return level


def gaussian(own_key, extent, scale, reach, shards=(), kind=jnp.bfloat16):
    entries = jax.random.normal(own_key, extent, jnp.float32) * scale
    if len(shards) > 0:
        entries = block_scale(own_key, extent, shards, -0.22, 0.18) * entries
    return jnp.clip(entries, min=-reach, max=reach).astype(kind)


def setup_inputs(seed: int = 0) -> dict:
    seeds = jax.random.split(jax.random.key(seed), 4)
    resident_keys = place_ends(jax.random.randint(seeds[0], (R_ROWS,), 0, KEYS), jax.random.fold_in(seeds[0], 1), 0, KEYS - 1).astype(jnp.int32)
    moving_keys = place_ends(jax.random.randint(seeds[1], (S_ROWS,), 0, KEYS), jax.random.fold_in(seeds[1], 1), 0, KEYS - 1).astype(jnp.int32)
    payload = gaussian(seeds[2], (S_ROWS, P_SIZE), 1.0, 6.0, ((0, 32),), jnp.float32)
    return {"resident_keys": resident_keys, "moving_keys": moving_keys, "payload": payload}


def match_block(res_keys, mov_keys, mov_pay):
    hot = (res_keys[:, None] == mov_keys[None, :]).astype(jnp.float32)
    return jnp.dot(hot, mov_pay, precision=lax.Precision.HIGHEST, preferred_element_type=jnp.float32)


def reference(resident_keys, moving_keys, payload):
    res_blocks = resident_keys.reshape(N_BLK, R_DEV)
    key_blocks = moving_keys.reshape(N_BLK, N_REP * S_DEV)
    pay_blocks = payload.reshape(N_BLK, N_REP * S_DEV, P_SIZE)

    def per_block(index):
        res_here = res_blocks[index]
        total = jnp.zeros((R_DEV, P_SIZE), jnp.float32)
        for offset in range(-REACH, REACH + 1):
            source = (index + offset) % N_BLK
            total = total + match_block(res_here, key_blocks[source], pay_blocks[source])
        return total

    joined = lax.map(per_block, jnp.arange(N_BLK, dtype=jnp.int32))
    return joined.reshape(N_BLK * R_DEV, P_SIZE)
```

```python
import functools

import jax
import jax.numpy as jnp
from jax import lax
from jax.experimental import pallas as pl
from jax.experimental.pallas import tpu as pltpu
from jax.sharding import PartitionSpec as P

REACH = 2
LANES = 128
CHUNK = 512


def kernel(
    n_blk, groups, rk_ref, mk_ref, pay_ref, out_ref,
    other_pay, mkeys, rkeys, hl, kcol, acc, abuf, xrecv, bbuf, sbuf, brecv,
    key_send, key_recv, pair_send, pair_recv, x_send, x_recv, b_send, b_recv,
):
    blk = lax.axis_index("blk")
    rep = lax.axis_index("rep")
    group, core = rep // 2, rep % 2
    rows = pay_ref.shape[0]
    width = pay_ref.shape[1]
    quarter = out_ref.shape[0]
    key_rows = mk_ref.shape[0]
    qrows = quarter // LANES
    par = blk % 2 if n_blk % 2 == 0 else 0
    near = 2 * par - 1
    offs = [REACH, -REACH, near, -near]
    key_to = [-REACH, REACH] + ([near, -near] if n_blk % 2 == 0 else [-near, near])
    slots = len(offs)

    def at(off):
        return lax.rem(blk + off + n_blk, n_blk)

    mate = rep + 1 - 2 * core
    peers = [lax.rem(group + d, groups) * 2 + core for d in range(1, groups)]

    barrier = pltpu.get_barrier_semaphore()
    pl.semaphore_signal(barrier, inc=1, device_id={"rep": mate})
    for p in peers:
        pl.semaphore_signal(barrier, inc=1, device_id={"rep": p})
    for o in offs:
        pl.semaphore_signal(barrier, inc=1, device_id={"blk": at(o)})
    mkeys[0:key_rows] = mk_ref[...]
    rkeys[slots] = rk_ref[...]
    pl.semaphore_wait(barrier, 1 + len(peers) + slots)

    sends = []
    pays = []
    pair_keys = pltpu.make_async_remote_copy(
        src_ref=mk_ref, dst_ref=mkeys.at[pl.ds(key_rows, key_rows)],
        send_sem=pair_send.at[0], recv_sem=pair_recv.at[0], device_id={"rep": mate})
    pair_keys.start()
    pair_pay = pltpu.make_async_remote_copy(
        src_ref=pay_ref, dst_ref=other_pay,
        send_sem=pair_send.at[1], recv_sem=pair_recv.at[1], device_id={"rep": mate})
    pair_pay.start()
    keys = []
    for i in range(slots):
        c = pltpu.make_async_remote_copy(
            src_ref=rk_ref, dst_ref=rkeys.at[i],
            send_sem=key_send.at[i], recv_sem=key_recv.at[i],
            device_id={"blk": at(key_to[i])})
        c.start()
        keys.append(c)

    def split(src, base):
        @pl.loop(0, rows // CHUNK)
        def _(k):
            v = src[pl.ds(k * CHUNK, CHUNK), :]
            hi = v.astype(jnp.bfloat16)
            lo = (v - hi.astype(jnp.float32)).astype(jnp.bfloat16)
            hl[pl.ds(base + k * CHUNK, CHUNK), 0:width] = hi
            hl[pl.ds(base + k * CHUNK, CHUNK), width:2 * width] = lo

    split(pay_ref, 0)
    pair_keys.wait_recv()
    pair_pay.wait_recv()
    split(other_pay, rows)

    def partial(slot, q, dst):
        for j in range(qrows):
            row = rkeys[slot, pl.ds(q * qrows + j, 1), :]
            kcol[j * LANES:(j + 1) * LANES, :] = jnp.broadcast_to(row, (LANES, LANES)).T
        acc[...] = jnp.zeros_like(acc)
        per = CHUNK // LANES

        @pl.loop(0, 2 * rows // CHUNK)
        def _(k):
            mine = kcol[...]
            hot = []
            for g in range(per):
                row = mkeys[pl.ds(k * per + g, 1), :]
                hot.append(jnp.where(mine == row, 1.0, 0.0).astype(jnp.bfloat16))
            hot = jnp.concatenate(hot, axis=1)
            acc[...] += jnp.dot(hot, hl[pl.ds(k * CHUNK, CHUNK), :],
                                preferred_element_type=jnp.float32)

        dst[...] = acc[:, 0:width] + acc[:, width:2 * width]

    x_copies = []
    b_copies = []

    def finish(i):
        total = bbuf[i]
        for d in range(groups - 1):
            x_copies[i][d].wait_recv()
            total = total + xrecv[i, d]
        if i == slots:
            return total
        sbuf[i] = total
        c = pltpu.make_async_remote_copy(
            src_ref=sbuf.at[i], dst_ref=brecv.at[i],
            send_sem=b_send.at[i], recv_sem=b_recv.at[i],
            device_id={"blk": at(offs[i])})
        c.start()
        b_copies.append(c)

    for i in range(slots + 1):
        if i < slots:
            keys[i].wait_recv()
        x_copies.append([])
        for d, p in enumerate(peers):
            partial(i, p, abuf.at[i, d])
            c = pltpu.make_async_remote_copy(
                src_ref=abuf.at[i, d], dst_ref=xrecv.at[i, d],
                send_sem=x_send.at[i, d], recv_sem=x_recv.at[i, d],
                device_id={"rep": p})
            c.start()
            x_copies[i].append(c)
        partial(i, rep, bbuf.at[i])
        if i >= 1:
            finish(i - 1)
    total = finish(slots)
    for i in range(slots):
        b_copies[i].wait_recv()
        total = total + brecv[i]
    out_ref[...] = total
    pair_keys.wait_send()
    pair_pay.wait_send()
    for c in keys + b_copies:
        c.wait_send()
    for row in x_copies:
        for c in row:
            c.wait_send()


def solution(mesh):
    n_blk, n_rep = mesh.shape["blk"], mesh.shape["rep"]
    groups = n_rep // 2
    slots = 4

    def local(resident_keys, moving_keys, payload):
        res, rows, width = resident_keys.shape[0], payload.shape[0], payload.shape[1]
        quarter = res // n_rep
        f32, bf16, i32 = jnp.float32, jnp.bfloat16, jnp.int32
        vmem = pl.BlockSpec(memory_space=pltpu.VMEM)
        dma = pltpu.SemaphoreType.DMA
        return pl.pallas_call(
            functools.partial(kernel, n_blk, groups),
            out_shape=jax.ShapeDtypeStruct((quarter, width), f32),
            in_specs=[vmem, vmem, vmem],
            out_specs=vmem,
            scratch_shapes=[
                pltpu.VMEM((rows, width), f32),
                pltpu.VMEM((2 * rows // LANES, LANES), i32),
                pltpu.VMEM((slots + 1, res // LANES, LANES), i32),
                pltpu.VMEM((2 * rows, 2 * width), bf16),
                pltpu.VMEM((quarter, LANES), i32),
                pltpu.VMEM((quarter, 2 * width), f32),
                pltpu.VMEM((slots + 1, groups - 1, quarter, width), f32),
                pltpu.VMEM((slots + 1, groups - 1, quarter, width), f32),
                pltpu.VMEM((slots + 1, quarter, width), f32),
                pltpu.VMEM((slots, quarter, width), f32),
                pltpu.VMEM((slots, quarter, width), f32),
                dma((slots,)), dma((slots,)),
                dma((2,)), dma((2,)),
                dma((slots + 1, groups - 1)), dma((slots + 1, groups - 1)),
                dma((slots,)), dma((slots,)),
            ],
            compiler_params=pltpu.CompilerParams(
                collective_id=0, has_side_effects=True, vmem_limit_bytes=48 * 1024 * 1024),
        )(resident_keys.reshape(res // LANES, LANES), moving_keys.reshape(rows // LANES, LANES), payload)

    in_specs = (P("blk"), P(("blk", "rep")), P(("blk", "rep"), None))
    out_specs = P(("blk", "rep"), None)
    return jax.shard_map(local, mesh=mesh, in_specs=in_specs, out_specs=out_specs, check_vma=False)
```

```python
import functools

import jax
import jax.numpy as jnp
from jax import lax
from jax.experimental import pallas as pl
from jax.experimental.pallas import tpu as pltpu
from jax.sharding import PartitionSpec as P

REACH = 2
LANES = 128
CHUNK = 2048


def kernel(
    n_blk, groups, rk_ref, mk_ref, pay_ref, out_ref,
    pay, other_pay, mkeys, rkeys, hl, kcol, abuf, xrecv, bbuf, sbuf, brecv, yrecv,
    in_sem, key_send, key_recv, pair_send, pair_recv, x_send, x_recv, b_send, b_recv, y_send, y_recv,
):
    blk = lax.axis_index("blk")
    rep = lax.axis_index("rep")
    group, core = rep // 2, rep % 2
    rows, width = pay.shape
    quarter = out_ref.shape[0]
    key_rows = mk_ref.shape[0]
    qrows = quarter // LANES
    fold = n_blk % 2 == 0
    near = 2 * (blk % 2) - 1 if fold else -1
    offs = [REACH, -REACH, near, -near]
    key_to = [-REACH, REACH] + ([near, -near] if fold else [-near, near])
    own = len(offs)

    def at(off):
        return lax.rem(blk + off + n_blk, n_blk)

    mate = rep + 1 - 2 * core
    peers = [lax.rem(group + d, groups) * 2 + core for d in range(1, groups)]

    load_pay = pltpu.make_async_copy(pay_ref, pay, in_sem.at[0])
    load_mk = pltpu.make_async_copy(mk_ref, mkeys.at[pl.ds(0, key_rows)], in_sem.at[1])
    load_rk = pltpu.make_async_copy(rk_ref, rkeys.at[own], in_sem.at[2])
    for c in (load_pay, load_mk, load_rk):
        c.start()

    barrier = pltpu.get_barrier_semaphore()
    for o in offs:
        pl.semaphore_signal(barrier, inc=1, device_id={"blk": at(o)})
    for p in peers + [mate]:
        pl.semaphore_signal(barrier, inc=1, device_id={"rep": p})
    pl.semaphore_wait(barrier, 1 + len(peers) + own)

    sent = []

    def send(src, dst, send_sem, recv_sem, to):
        c = pltpu.make_async_remote_copy(
            src_ref=src, dst_ref=dst, send_sem=send_sem, recv_sem=recv_sem, device_id=to)
        c.start()
        sent.append(c)
        return c

    keys = {}
    for i in (0, 3, 2, 1):
        keys[i] = send(rk_ref, rkeys.at[i], key_send.at[i], key_recv.at[i], {"blk": at(key_to[i])})
    pair_keys = send(mk_ref, mkeys.at[pl.ds(key_rows, key_rows)], pair_send.at[0], pair_recv.at[0], {"rep": mate})
    pair_pay = send(pay_ref, other_pay, pair_send.at[1], pair_recv.at[1], {"rep": mate})

    def split(src, base):
        @pl.loop(0, rows // 256)
        def _(k):
            v = src[pl.ds(k * 256, 256), :]
            hi = v.astype(jnp.bfloat16)
            lo = (v - hi.astype(jnp.float32)).astype(jnp.bfloat16)
            hl[pl.ds(base + k * 256, 256), 0:width] = hi
            hl[pl.ds(base + k * 256, 256), width:2 * width] = lo

    for c in (load_pay, load_mk, load_rk):
        c.wait()
    split(pay, 0)
    pair_keys.wait_recv()
    pair_pay.wait_recv()
    split(other_pay, rows)

    per = CHUNK // LANES

    def partial(slot, q):
        for j in range(qrows):
            row = rkeys[slot, pl.ds(q * qrows + j, 1), :]
            kcol[j * LANES:(j + 1) * LANES, :] = jnp.broadcast_to(row, (LANES, LANES)).T

        def part(k):
            mine = kcol[...]
            hot = []
            for g in range(per):
                row = mkeys[pl.ds(k * per + g, 1), :]
                hot.append(jnp.where(mine == row, 1.0, 0.0).astype(jnp.bfloat16))
            both = jnp.dot(jnp.concatenate(hot, axis=1), hl[pl.ds(k * CHUNK, CHUNK), :],
                           preferred_element_type=jnp.float32)
            return both[:, 0:width] + both[:, width:2 * width]

        return part, 2 * rows // CHUNK

    def compute(slot, q, dst):
        part, steps = partial(slot, q)
        if steps == 1:
            dst[...] = part(0)
            return
        dst[...] = part(0)

        @pl.loop(1, steps)
        def _(k):
            dst[...] += part(k)

    waiting = {}

    def send_x(i):
        waiting[i] = [
            send(abuf.at[i, d], xrecv.at[i, d], x_send.at[i, d], x_recv.at[i, d], {"rep": p})
            for d, p in enumerate(peers)]

    ready = set()

    def for_peers(i):
        if i != own and i not in ready:
            keys[i].wait_recv()
            ready.add(i)
        for d, p in enumerate(peers):
            compute(i, p, abuf.at[i, d])

    def for_me(i):
        compute(i, rep, bbuf.at[i])

    def finish(i):
        total = bbuf[i]
        for d, c in enumerate(waiting[i]):
            c.wait_recv()
            total = total + xrecv[i, d]
        return total

    def give(i):
        sbuf[i] = finish(i)
        return send(sbuf.at[i], brecv.at[i], b_send.at[i], b_recv.at[i], {"blk": at(offs[i])})

    def give_partner(src, d):
        return send(src, yrecv.at[d], y_send.at[d], y_recv.at[d], {"blk": at(offs[3])})

    for_peers(0)
    send_x(0)
    for_peers(3)
    if fold:
        folded = [give_partner(abuf.at[3, d], d) for d in range(groups - 1)]
    else:
        send_x(3)
    for_me(0)
    for_peers(2)
    send_x(2)
    given = [give(0)]
    for_peers(1)
    send_x(1)
    for_me(3)
    if fold:
        last = give_partner(bbuf.at[3], groups - 1)
    for_me(2)
    for_peers(own)
    if fold:
        for d, c in enumerate(folded):
            c.wait_recv()
            abuf[own, d] = abuf[own, d] + yrecv[d]
    send_x(own)
    given.append(give(2))
    for_me(1)
    if not fold:
        given.append(give(3))
    for_me(own)
    given.append(give(1))
    total = bbuf[own]
    if fold:
        last.wait_recv()
        total = total + yrecv[groups - 1]
    bbuf[own] = total
    total = finish(own)
    for i, c in zip((0, 2, 1) if fold else (0, 2, 3, 1), given):
        c.wait_recv()
        total = total + brecv[i]
    out_ref[...] = total
    for c in sent:
        c.wait_send()


def solution(mesh):
    n_blk, n_rep = mesh.shape["blk"], mesh.shape["rep"]
    groups = n_rep // 2
    slots = 4

    def local(resident_keys, moving_keys, payload):
        res, rows, width = resident_keys.shape[0], payload.shape[0], payload.shape[1]
        quarter = res // n_rep
        f32, bf16, i32 = jnp.float32, jnp.bfloat16, jnp.int32
        vmem = pl.BlockSpec(memory_space=pltpu.VMEM)
        dma = pltpu.SemaphoreType.DMA
        return pl.pallas_call(
            functools.partial(kernel, n_blk, groups),
            out_shape=jax.ShapeDtypeStruct((quarter, width), f32),
            in_specs=[pl.BlockSpec(memory_space=pl.ANY)] * 3,
            out_specs=vmem,
            scratch_shapes=[
                pltpu.VMEM((rows, width), f32),
                pltpu.VMEM((rows, width), f32),
                pltpu.VMEM((2 * rows // LANES, LANES), i32),
                pltpu.VMEM((slots + 1, res // LANES, LANES), i32),
                pltpu.VMEM((2 * rows, 2 * width), bf16),
                pltpu.VMEM((quarter, LANES), i32),
                pltpu.VMEM((slots + 1, groups - 1, quarter, width), f32),
                pltpu.VMEM((slots + 1, groups - 1, quarter, width), f32),
                pltpu.VMEM((slots + 1, quarter, width), f32),
                pltpu.VMEM((slots, quarter, width), f32),
                pltpu.VMEM((slots, quarter, width), f32),
                pltpu.VMEM((groups, quarter, width), f32),
                dma((3,)),
                dma((slots,)), dma((slots,)),
                dma((2,)), dma((2,)),
                dma((slots + 1, groups - 1)), dma((slots + 1, groups - 1)),
                dma((slots,)), dma((slots,)),
                dma((groups,)), dma((groups,)),
            ],
            compiler_params=pltpu.CompilerParams(
                collective_id=0, has_side_effects=True, vmem_limit_bytes=48 * 1024 * 1024),
        )(resident_keys.reshape(res // LANES, LANES), moving_keys.reshape(rows // LANES, LANES), payload)

    in_specs = (P("blk"), P(("blk", "rep")), P(("blk", "rep"), None))
    out_specs = P(("blk", "rep"), None)
    return jax.shard_map(local, mesh=mesh, in_specs=in_specs, out_specs=out_specs, check_vma=False)
```

```python
import functools

import jax
import jax.numpy as jnp
from jax import lax
from jax.experimental import pallas as pl
from jax.experimental.pallas import tpu as pltpu
from jax.sharding import PartitionSpec as P

REACH = 2
LANES = 128
CHUNK = 2048


def kernel(
    n_blk, groups, rk_ref, mk_ref, pay_ref, out_ref,
    pay, other_pay, mkeys, rkeys, hl, kcol, abuf, xrecv, bbuf, sbuf, brecv, yrecv,
    in_sem, key_send, key_recv, pair_send, pair_recv, x_send, x_recv, b_send, b_recv, y_send, y_recv,
):
    blk = lax.axis_index("blk")
    rep = lax.axis_index("rep")
    group, core = rep // 2, rep % 2
    rows, width = pay.shape
    quarter = out_ref.shape[0]
    key_rows = mk_ref.shape[0]
    qrows = quarter // LANES
    fold = n_blk % 2 == 0
    near = 2 * (blk % 2) - 1 if fold else -1
    offs = [REACH, -REACH, near, -near]
    key_to = [-REACH, REACH] + ([near, -near] if fold else [-near, near])
    own = len(offs)

    def at(off):
        return lax.rem(blk + off + n_blk, n_blk)

    mate = rep + 1 - 2 * core
    peers = [lax.rem(group + d, groups) * 2 + core for d in range(1, groups)]

    load_pay = pltpu.make_async_copy(pay_ref, pay, in_sem.at[0])
    load_mk = pltpu.make_async_copy(mk_ref, mkeys.at[pl.ds(0, key_rows)], in_sem.at[1])
    load_rk = pltpu.make_async_copy(rk_ref, rkeys.at[own], in_sem.at[2])
    for c in (load_pay, load_mk, load_rk):
        c.start()

    barrier = pltpu.get_barrier_semaphore()
    for o in offs:
        pl.semaphore_signal(barrier, inc=1, device_id={"blk": at(o)})
    for p in peers + [mate]:
        pl.semaphore_signal(barrier, inc=1, device_id={"rep": p})
    def split(src, base):
        @pl.loop(0, rows // 256)
        def _(k):
            v = src[pl.ds(k * 256, 256), :]
            hi = v.astype(jnp.bfloat16)
            lo = (v - hi.astype(jnp.float32)).astype(jnp.bfloat16)
            hl[pl.ds(base + k * 256, 256), 0:width] = hi
            hl[pl.ds(base + k * 256, 256), width:2 * width] = lo

    for c in (load_pay, load_mk, load_rk):
        c.wait()
    split(pay, 0)
    pl.semaphore_wait(barrier, 1 + len(peers) + own)

    sent = []

    def send(src, dst, send_sem, recv_sem, to):
        c = pltpu.make_async_remote_copy(
            src_ref=src, dst_ref=dst, send_sem=send_sem, recv_sem=recv_sem, device_id=to)
        c.start()
        sent.append(c)
        return c

    keys = {}
    for i in (0, 3, 2, 1):
        keys[i] = send(rk_ref, rkeys.at[i], key_send.at[i], key_recv.at[i], {"blk": at(key_to[i])})
    pair_keys = send(mk_ref, mkeys.at[pl.ds(key_rows, key_rows)], pair_send.at[0], pair_recv.at[0], {"rep": mate})
    pair_pay = send(pay_ref, other_pay, pair_send.at[1], pair_recv.at[1], {"rep": mate})

    per = CHUNK // LANES

    def partial(slot, q):
        for j in range(qrows):
            row = rkeys[slot, pl.ds(q * qrows + j, 1), :]
            kcol[j * LANES:(j + 1) * LANES, :] = jnp.broadcast_to(row, (LANES, LANES)).T

        def part(k):
            mine = kcol[...]
            hot = []
            for g in range(per):
                row = mkeys[pl.ds(k * per + g, 1), :]
                hot.append(jnp.where(mine == row, 1.0, 0.0).astype(jnp.bfloat16))
            both = jnp.dot(jnp.concatenate(hot, axis=1), hl[pl.ds(k * CHUNK, CHUNK), :],
                           preferred_element_type=jnp.float32)
            return both[:, 0:width] + both[:, width:2 * width]

        return part

    def compute(slot, q, dst, first=0, last=2 * rows // CHUNK):
        part = partial(slot, q)
        if first == 0:
            dst[...] = part(0)

        @pl.loop(max(first, 1), last)
        def _(k):
            dst[...] += part(k)

    compute(own, rep, bbuf.at[own], last=rows // CHUNK)
    pair_keys.wait_recv()
    pair_pay.wait_recv()
    split(other_pay, rows)

    waiting = {}

    def send_x(i):
        waiting[i] = [
            send(abuf.at[i, d], xrecv.at[i, d], x_send.at[i, d], x_recv.at[i, d], {"rep": p})
            for d, p in enumerate(peers)]

    ready = set()

    def for_peers(i):
        if i != own and i not in ready:
            keys[i].wait_recv()
            ready.add(i)
        for d, p in enumerate(peers):
            compute(i, p, abuf.at[i, d])

    def for_me(i):
        compute(i, rep, bbuf.at[i])

    def finish(i):
        total = bbuf[i]
        for d, c in enumerate(waiting[i]):
            c.wait_recv()
            total = total + xrecv[i, d]
        return total

    def give(i):
        sbuf[i] = finish(i)
        return send(sbuf.at[i], brecv.at[i], b_send.at[i], b_recv.at[i], {"blk": at(offs[i])})

    def give_partner(src, d):
        return send(src, yrecv.at[d], y_send.at[d], y_recv.at[d], {"blk": at(offs[3])})

    for_peers(0)
    send_x(0)
    for_peers(3)
    if fold:
        folded = [give_partner(abuf.at[3, d], d) for d in range(groups - 1)]
    else:
        send_x(3)
    for_me(0)
    for_peers(2)
    send_x(2)
    given = [give(0)]
    for_peers(1)
    send_x(1)
    for_me(3)
    if fold:
        last = give_partner(bbuf.at[3], groups - 1)
    for_me(2)
    for_peers(own)
    if fold:
        for d, c in enumerate(folded):
            c.wait_recv()
            abuf[own, d] = abuf[own, d] + yrecv[d]
    send_x(own)
    given.append(give(2))
    for_me(1)
    if not fold:
        given.append(give(3))
    compute(own, rep, bbuf.at[own], first=rows // CHUNK)
    given.append(give(1))
    total = bbuf[own]
    if fold:
        last.wait_recv()
        total = total + yrecv[groups - 1]
    bbuf[own] = total
    total = finish(own)
    for i, c in zip((0, 2, 1) if fold else (0, 2, 3, 1), given):
        c.wait_recv()
        total = total + brecv[i]
    out_ref[...] = total
    for c in sent:
        c.wait_send()


def solution(mesh):
    n_blk, n_rep = mesh.shape["blk"], mesh.shape["rep"]
    groups = n_rep // 2
    slots = 4

    def local(resident_keys, moving_keys, payload):
        res, rows, width = resident_keys.shape[0], payload.shape[0], payload.shape[1]
        quarter = res // n_rep
        f32, bf16, i32 = jnp.float32, jnp.bfloat16, jnp.int32
        vmem = pl.BlockSpec(memory_space=pltpu.VMEM)
        dma = pltpu.SemaphoreType.DMA
        return pl.pallas_call(
            functools.partial(kernel, n_blk, groups),
            out_shape=jax.ShapeDtypeStruct((quarter, width), f32),
            in_specs=[pl.BlockSpec(memory_space=pl.ANY)] * 3,
            out_specs=vmem,
            scratch_shapes=[
                pltpu.VMEM((rows, width), f32),
                pltpu.VMEM((rows, width), f32),
                pltpu.VMEM((2 * rows // LANES, LANES), i32),
                pltpu.VMEM((slots + 1, res // LANES, LANES), i32),
                pltpu.VMEM((2 * rows, 2 * width), bf16),
                pltpu.VMEM((quarter, LANES), i32),
                pltpu.VMEM((slots + 1, groups - 1, quarter, width), f32),
                pltpu.VMEM((slots + 1, groups - 1, quarter, width), f32),
                pltpu.VMEM((slots + 1, quarter, width), f32),
                pltpu.VMEM((slots, quarter, width), f32),
                pltpu.VMEM((slots, quarter, width), f32),
                pltpu.VMEM((groups, quarter, width), f32),
                dma((3,)),
                dma((slots,)), dma((slots,)),
                dma((2,)), dma((2,)),
                dma((slots + 1, groups - 1)), dma((slots + 1, groups - 1)),
                dma((slots,)), dma((slots,)),
                dma((groups,)), dma((groups,)),
            ],
            compiler_params=pltpu.CompilerParams(
                collective_id=0, has_side_effects=True, vmem_limit_bytes=48 * 1024 * 1024),
        )(resident_keys.reshape(res // LANES, LANES), moving_keys.reshape(rows // LANES, LANES), payload)

    in_specs = (P("blk"), P(("blk", "rep")), P(("blk", "rep"), None))
    out_specs = P(("blk", "rep"), None)
    return jax.shard_map(local, mesh=mesh, in_specs=in_specs, out_specs=out_specs, check_vma=False)
```
